32 devices in a mesh: design: 2 (over x), domain: 16 (over z, y, core).
Axes of the slice: x: 2, y: 2, z: 4, core: 2. Of those that a mesh axis runs over, the one named last changes fastest.
Arguments:
- e_field: float32 [3, 128, 64, 128], P(None, ('design', 'domain')), parts along dimension 1, may hold values from -6 to 6
- h_field: float32 [3, 128, 64, 128], P(None, ('design', 'domain')), parts along dimension 1, may hold values from -6 to 6
- adj_e_field: float32 [3, 128, 64, 128], P(None, ('design', 'domain')), parts along dimension 1, may hold values from -6 to 6
- adj_h_field: float32 [3, 128, 64, 128], P(None, ('design', 'domain')), parts along dimension 1, may hold values from -6 to 6
- permittivity: float32 [3, 256], P(None, ('design', 'domain')), parts along dimension 1, may hold values from 1 to 6
- conductivity: float32 [3, 256], P(None, ('design', 'domain')), parts along dimension 1, may hold values from 0.02 to 0.6
- region_labels: int32 [128, 8, 16], P(('design', 'domain')), parts along dimension 0, may hold values from 0 to 127
- source_plane: int32 [2], P('design'), parts along dimension 0, may hold values from 0 to 63
- monitor_plane: int32 [2], P('design'), parts along dimension 0, may hold values from 0 to 63
- wave_index: int32 [8], P('design'), parts along dimension 0, may hold values from 0 to 15
- source_mode: float32 [128, 128], P('design'), parts along dimension 0, may hold values from -6 to 6
- monitor_mode: float32 [128, 128], P('design'), parts along dimension 0, may hold values from -6 to 6
Outputs:
- region_grads: float32 [6, 256], P(None, ('design', 'domain')), parts along dimension 1
The draws below stay inside these ranges and needn't reach their ends.
There are 2 independent parts, one for each index of `design`. The reference program is written for one: setup_inputs(seed, part) draws one part's arguments, and reference() takes and returns one part's arrays. A program takes and returns all parts, laid end to end along the dimension named above; each array names one. Nothing has to cross between parts.
All inputs are finite; a program needn't handle non-finite values.
Results may differ from the reference program's by a relative error of at most 0.0003.
Values sent between devices are 32-bit elements; how exact they have to be, the bound alone decides.
A program may use at most 64 MiB of HBM per device.

```python
import math
import jax
import jax.numpy as jnp
from jax import lax

NY = 64
NZ = 128
STEPS = 8
NF = 4
NWAVE = 16
NX = 64
REGIONS = 128


def place_ends(array, key, smallest, top_value):
    extent = array.shape
    index_at = [jax.random.randint(jax.random.fold_in(key, axis), (), 0, extent[axis]) for axis in range(len(extent))]
    array = array.at[tuple(index_at)].set(smallest)
    longest = extent.index(max(extent))
    index_at[longest] = (index_at[longest] + 1) % extent[longest]
    return array.at[tuple(index_at)].set(top_value)


def steps_of(stream_key, dims, split, smallest, top_value):
    def one(axis_at, parts):
        draws = jax.random.uniform(jax.random.fold_in(jax.random.fold_in(stream_key, 6), axis_at), (parts,), jnp.float32, smallest / len(split), top_value / len(split))
        return jnp.repeat(jnp.exp(draws), dims[axis_at] // parts).reshape((-1,) + (1,) * (len(dims) - axis_at - 1))

    level = one(*split[0])
    for cut in split[1:]:
        level = level * one(*cut)
    return level


def normal_values(key, shape, width, most, split=(), kind=jnp.bfloat16):
    loudness = steps_of(key, shape, split, -0.22, 0.18) if split else 1.0
    entries = jax.random.normal(key, shape, jnp.float32) * width * loudness
    return jnp.minimum(jnp.maximum(entries, -most), most).astype(kind)


def setup_inputs(seed: int = 0, part: int = 0) -> dict:
    streams_of = jax.random.split(jax.random.key(seed), 13)
    part_splits = jax.random.split(jax.random.fold_in(streams_of[12], part), 13)
    e_field = normal_values(part_splits[0], (3, NX, NY, NZ), 1.0, 6.0, ((1, 16),), jnp.float32)
    h_field = normal_values(part_splits[1], (3, NX, NY, NZ), 1.0, 6.0, ((1, 16),), jnp.float32)
    adj_e_field = normal_values(part_splits[2], (3, NX, NY, NZ), 1.0, 6.0, ((1, 16),), jnp.float32)
    adj_h_field = normal_values(part_splits[3], (3, NX, NY, NZ), 1.0, 6.0, ((1, 16),), jnp.float32)
    permittivity = jnp.clip(1.0 + 5.0 * jax.random.uniform(part_splits[4], (3, REGIONS), jnp.float32) ** steps_of(part_splits[4], (3, REGIONS), ((1, 16),), -0.2, 0.2), 1.0, 6.0)
    conductivity = jnp.clip(jnp.exp(math.log(0.6) - 3.4011974 * jax.random.uniform(part_splits[5], (3, REGIONS), jnp.float32) ** steps_of(part_splits[5], (3, REGIONS), ((1, 16),), -0.2, 0.2)), 0.02, 0.6)
    region_labels = place_ends(jax.random.randint(part_splits[6], (NX, NY // 8, NZ // 8), 0, REGIONS), jax.random.fold_in(part_splits[6], 1), 0, REGIONS - 1).astype(jnp.int32)
    source_plane = jax.random.randint(part_splits[7], (1,), 0, NX).astype(jnp.int32)
    monitor_plane = jax.random.randint(part_splits[8], (1,), 0, NX).astype(jnp.int32)
    wave_index = place_ends(jax.random.randint(part_splits[9], (NF,), 0, NWAVE), jax.random.fold_in(part_splits[9], 1), 0, NWAVE - 1).astype(jnp.int32)
    source_mode = normal_values(part_splits[10], (NY, NZ), 1.0, 6.0, (), jnp.float32)
    monitor_mode = normal_values(part_splits[11], (NY, NZ), 1.0, 6.0, (), jnp.float32)
    return dict(e_field=e_field, h_field=h_field, adj_e_field=adj_e_field, adj_h_field=adj_h_field, permittivity=permittivity, conductivity=conductivity, region_labels=region_labels, source_plane=source_plane, monitor_plane=monitor_plane, wave_index=wave_index, source_mode=source_mode, monitor_mode=monitor_mode)


COURANT = 0.5

def lagged(values, axis):
    zero = jnp.zeros_like(lax.slice_in_dim(values, 0, 1, axis=axis))
    return jnp.concatenate([zero, lax.slice_in_dim(values, 0, values.shape[axis] - 1, axis=axis)], axis=axis)

def leading(values, axis):
    zero = jnp.zeros_like(lax.slice_in_dim(values, 0, 1, axis=axis))
    return jnp.concatenate([lax.slice_in_dim(values, 1, values.shape[axis], axis=axis), zero], axis=axis)

def new_electric(electric, magnetic, hy_left, hz_left, keep_rate, gain_rate, forcing, component):
    curl_x = magnetic[2] - lagged(magnetic[2], 1) - (magnetic[1] - lagged(magnetic[1], 2))
    curl_y = magnetic[0] - lagged(magnetic[0], 2) - (magnetic[2] - hz_left)
    curl_z = magnetic[1] - hy_left - (magnetic[0] - lagged(magnetic[0], 1))
    curls = (curl_x, curl_y, curl_z)
    updated = []
    for c in range(3):
        pushing = COURANT * curls[c]
        if c == component:
            pushing = pushing - forcing
        updated.append(keep_rate[c] * electric[c] + gain_rate[c] * pushing)
    return jnp.stack(updated)

def new_magnetic(magnetic, electric, ey_right, ez_right):
    curl_x = leading(electric[2], 1) - electric[2] - (leading(electric[1], 2) - electric[1])
    curl_y = leading(electric[0], 2) - electric[0] - (ez_right - electric[2])
    curl_z = ey_right - electric[1] - (leading(electric[0], 1) - electric[0])
    return jnp.stack([magnetic[0] - COURANT * curl_x, magnetic[1] - COURANT * curl_y, magnetic[2] - COURANT * curl_z])

def spread(blocks):
    shape = blocks.shape
    grown = jnp.broadcast_to(blocks[:, :, :, None, :, None], (shape[0], shape[1], shape[2], 8, shape[3], 8))
    return grown.reshape(shape[0], shape[1], shape[2] * 8, shape[3] * 8)

def evolve(electric, magnetic, keep_rate, gain_rate, profile, component, amp_cos, amp_sin, omega):
    spectra_re = jnp.zeros((omega.shape[0],) + electric.shape, jnp.float32)
    spectra_im = jnp.zeros((omega.shape[0],) + electric.shape, jnp.float32)
    for step in range(STEPS):
        moment = jnp.float32(step + 1)
        cosines = jnp.cos(omega * moment)
        sines = jnp.sin(omega * moment)
        forcing = profile * jnp.sum(amp_cos * cosines + amp_sin * sines)
        electric = new_electric(electric, magnetic, lagged(magnetic[1], 0), lagged(magnetic[2], 0), keep_rate, gain_rate, forcing, component)
        magnetic = new_magnetic(magnetic, electric, leading(electric[1], 0), leading(electric[2], 0))
        spectra_re = spectra_re + cosines[:, None, None, None, None] * electric[None]
        spectra_im = spectra_im - sines[:, None, None, None, None] * electric[None]
    return (spectra_re, spectra_im)

def reference(e_field, h_field, adj_e_field, adj_h_field, permittivity, conductivity, region_labels, source_plane, monitor_plane, wave_index, source_mode, monitor_mode):
    omega = 0.25 + 0.05 * wave_index.astype(jnp.float32)
    perm_blocks = permittivity[:, region_labels]
    cond_blocks = conductivity[:, region_labels]
    loss = cond_blocks * 0.5 / perm_blocks
    keep_rate = spread((1.0 - loss) / (1.0 + loss))
    gain_rate = spread(1.0 / (perm_blocks * (1.0 + loss)))
    layers = jnp.arange(NX, dtype=jnp.int32)[:, None, None]
    source_profile = jnp.where(layers == source_plane[0], source_mode[None], 0.0)
    monitor_profile = jnp.where(layers == monitor_plane[0], monitor_mode[None], 0.0)
    zeros_amp = jnp.zeros((NF,), jnp.float32)
    ones_amp = jnp.ones((NF,), jnp.float32)
    fwd_re, fwd_im = evolve(e_field, h_field, keep_rate, gain_rate, source_profile, 2, zeros_amp, ones_amp, omega)
    root = math.sqrt(NY * NZ)
    mon_re = fwd_re[:, 1, monitor_plane[0]]
    mon_im = fwd_im[:, 1, monitor_plane[0]]
    intersection_re = lax.optimization_barrier(jnp.sum(mon_re * monitor_mode, axis=(1, 2))) / root
    intersection_im = lax.optimization_barrier(jnp.sum(mon_im * monitor_mode, axis=(1, 2))) / root
    src_re = fwd_re[:, 2, source_plane[0]]
    src_im = fwd_im[:, 2, source_plane[0]]
    power = lax.optimization_barrier(jnp.mean(src_re * src_re + src_im * src_im, axis=(1, 2)))
    scale = 1.0 / jnp.sqrt(power + 1e-06)
    adj_re, adj_im = evolve(adj_e_field, adj_h_field, keep_rate, gain_rate, monitor_profile, 1, intersection_re * scale, intersection_im * scale, omega)
    squared = omega * omega
    grad_perm = lax.optimization_barrier(jnp.sum(squared[:, None, None, None, None] * (fwd_re * adj_re - fwd_im * adj_im), axis=0))
    grad_cond = lax.optimization_barrier(jnp.sum(omega[:, None, None, None, None] * (fwd_re * adj_im + fwd_im * adj_re), axis=0))
    cellwise = jnp.concatenate([grad_perm, grad_cond], 0)
    blocks = cellwise.reshape(6, NX, NY // 8, 8, NZ // 8, 8).sum(axis=(3, 5))
    per_region = jax.ops.segment_sum(blocks.reshape(6, -1).T, region_labels.reshape(-1), num_segments=REGIONS).T
    return per_region * math.sqrt(REGIONS / (NX * NY * NZ))
```

```python
import functools
import math

import jax
import jax.numpy as jnp
from jax import lax
from jax.experimental import pallas as pl
from jax.experimental.pallas import tpu as pltpu
from jax.sharding import PartitionSpec as P

STEPS = 8
NF = 4
MESH = pl.DeviceIdType.MESH
HIGH = lax.Precision.HIGHEST


def kernel(
    nd,
    planes_ref,
    coef_ref,
    e_hbm,
    h_hbm,
    ae_hbm,
    ah_hbm,
    tab_ref,
    lab_ref,
    packed_ref,
    src_ref,
    mon_ref,
    out_ref,
    hist,
    mag,
    send_r,
    send_l,
    recv_r,
    recv_l,
    rates,
    ghost,
    green,
    green_h,
    green_rates,
    tabs,
    labs,
    mids,
    ends,
    cells,
    tab_all,
    mid_own,
    end_own,
    load_sem,
    sr_sem,
    sl_sem,
    rr_sem,
    rl_sem,
    g_send,
    g_recv,
):
    width = lab_ref.shape[0]
    rows, lanes = src_ref.shape
    blocks = rows // 8
    regions = tab_ref.shape[1]
    per = regions // nd
    layers = nd * width
    me = lax.axis_index("domain")
    last = width - 1
    reach = STEPS - 1
    source = planes_ref[0]
    monitor = planes_ref[1]

    loads = []
    for r, (e, h) in enumerate(((e_hbm, h_hbm), (ae_hbm, ah_hbm))):
        loads.append(pltpu.make_async_copy(e, hist.at[r, 0], load_sem.at[2 * r]))
        loads.append(pltpu.make_async_copy(h, mag.at[r], load_sem.at[2 * r + 1]))
    for load in loads:
        load.start()

    barrier = pltpu.get_barrier_semaphore()

    def greet(j, carry):
        pl.semaphore_signal(
            barrier, inc=1, device_id={"domain": lax.rem(me + j, nd)}, device_id_type=MESH
        )
        return carry

    lax.fori_loop(1, nd, greet, 0)

    def to_all(phase, own, slots):
        def copy(j, away):
            return pltpu.make_async_remote_copy(
                src_ref=own,
                dst_ref=slots.at[away],
                send_sem=g_send.at[phase, j],
                recv_sem=g_recv.at[phase, j],
                device_id={"domain": lax.rem(me + j, nd)},
                device_id_type=MESH,
            )

        def begin():
            def one(j, carry):
                copy(j, me).start()
                return carry

            lax.fori_loop(1, nd, one, 0)

        def end():
            def one(j, carry):
                copy(j, me).wait_send()
                copy(j, lax.rem(me + nd - j, nd)).wait_recv()
                return carry

            lax.fori_loop(1, nd, one, 0)

        return begin, end

    tab_begin, tab_end = to_all(0, tab_ref, tabs)
    lab_begin, lab_end = to_all(1, lab_ref, labs)
    mid_begin, mid_end = to_all(2, mid_own, mids)
    end_begin, end_end = to_all(3, end_own, ends)

    pl.semaphore_wait(barrier, nd - 1)
    tab_begin()
    lab_begin()
    tabs[me] = tab_ref[...]
    labs[me] = lab_ref[...]

    row_at = lax.broadcasted_iota(jnp.int32, (rows, lanes), 0)
    lane_at = lax.broadcasted_iota(jnp.int32, (rows, lanes), 1)

    def lag_j(x):
        return jnp.where(row_at == 0, 0.0, pltpu.roll(x, 1, 0))

    def lag_k(x):
        return jnp.where(lane_at == 0, 0.0, pltpu.roll(x, 1, 1))

    def lead_j(x):
        return jnp.where(row_at == rows - 1, 0.0, pltpu.roll(x, rows - 1, 0))

    def lead_k(x):
        return jnp.where(lane_at == lanes - 1, 0.0, pltpu.roll(x, lanes - 1, 1))

    @pl.when(me == 0)
    def _():
        recv_r[...] = jnp.zeros_like(recv_r)

    @pl.when(me == nd - 1)
    def _():
        recv_l[...] = jnp.zeros_like(recv_l)

    def clear(w, carry):
        zero = jnp.zeros((rows, lanes), jnp.float32)
        for k in range(STEPS):
            for c in range(3):
                green[k, c, w] = zero
        for c in range(3):
            green_h[c, w] = zero
        return carry

    lax.fori_loop(0, 2 * reach + 3, clear, 0)

    tab_end()
    lab_end()

    def add_tab(s, acc):
        return acc + tabs[s]

    tab_all[...] = lax.fori_loop(1, nd, add_tab, tabs[0])

    def looked_up(c, label):
        value = jnp.zeros(label.shape, jnp.float32)
        for q in range(regions // lanes):
            row = jnp.broadcast_to(tab_all[c : c + 1, q * lanes : (q + 1) * lanes], label.shape)
            found = jnp.take_along_axis(row, lax.rem(label, lanes), axis=1)
            value = jnp.where(lax.div(label, lanes) == q, found, value)
        return value

    def rates_of(c, label):
        perm = looked_up(c, label)
        cond = looked_up(3 + c, label)
        loss = cond * 0.5 / perm
        return (1.0 - loss) / (1.0 + loss), 1.0 / (perm * (1.0 + loss))

    def spread(write, value):
        for b in range(blocks):
            write(b, jnp.broadcast_to(value[b : b + 1], (8, lanes)))

    for l in range(width):
        for c in range(3):
            keep, gain = rates_of(c, lab_ref[l])

            def put(b, v, c=c, l=l):
                rates[c, l, pl.ds(b * 8, 8)] = v

            def put_gain(b, v, c=c, l=l):
                rates[3 + c, l, pl.ds(b * 8, 8)] = v

            spread(put, keep)
            spread(put_gain, gain)

    after = lax.rem(me + 1, nd)
    inside = jnp.where(me == nd - 1, 0.0, 0.5)
    for c in (1, 2):
        _, gain = rates_of(c, labs[after, 0])

        def put_ghost(b, v, c=c):
            ghost[c - 1, pl.ds(b * 8, 8)] = v * inside

        spread(put_ghost, gain)

    for load in loads:
        load.wait()

    def forcing_at(n, l):
        lit = jnp.where(source == me * width + l, coef_ref[2, n], 0.0)
        return src_ref[...] * lit

    def make_edge(r, n):
        for c in (1, 2):
            send_r[r, n, c - 1] = mag[r, c, last]
        hx, hy, hz = mag[r, 0, 0], mag[r, 1, 0], mag[r, 2, 0]
        py = rates[1, 0] * hist[r, n, 1, 0] + rates[4, 0] * (0.5 * (hx - lag_k(hx) - hz))
        push = 0.5 * (hy - (hx - lag_j(hx)))
        if r == 0:
            push = push - forcing_at(n, 0)
        pz = rates[2, 0] * hist[r, n, 2, 0] + rates[5, 0] * push
        send_l[r, n, 0] = py
        send_l[r, n, 1] = pz

    def right_copy(r, n):
        return pltpu.make_async_remote_copy(
            src_ref=send_r.at[r, n],
            dst_ref=recv_r.at[r, n],
            send_sem=sr_sem.at[r, n],
            recv_sem=rr_sem.at[r, n],
            device_id={"domain": lax.rem(me + 1, nd)},
            device_id_type=MESH,
        )

    def left_copy(r, n):
        return pltpu.make_async_remote_copy(
            src_ref=send_l.at[r, n],
            dst_ref=recv_l.at[r, n],
            send_sem=sl_sem.at[r, n],
            recv_sem=rl_sem.at[r, n],
            device_id={"domain": lax.rem(me + nd - 1, nd)},
            device_id_type=MESH,
        )

    def start_edge(r, n):
        @pl.when(me < nd - 1)
        def _():
            right_copy(r, n).start()

        @pl.when((me > 0) & (n < STEPS - 1))
        def _():
            left_copy(r, n).start()

    def wait_right(r, n):
        @pl.when(me > 0)
        def _():
            right_copy(r, n).wait_recv()

    def wait_left(r, n):
        @pl.when(me < nd - 1)
        def _():
            left_copy(r, n).wait_recv()

    def electric_inner(r, n):
        for l in range(width):
            hx, hy, hz = mag[r, 0, l], mag[r, 1, l], mag[r, 2, l]
            hist[r, n + 1, 0, l] = rates[0, l] * hist[r, n, 0, l] + rates[3, l] * (
                0.5 * (hz - lag_j(hz) - (hy - lag_k(hy)))
            )
            if l == 0:
                continue
            hist[r, n + 1, 1, l] = rates[1, l] * hist[r, n, 1, l] + rates[4, l] * (
                0.5 * (hx - lag_k(hx) - (hz - mag[r, 2, l - 1]))
            )
            push = 0.5 * (hy - mag[r, 1, l - 1] - (hx - lag_j(hx)))
            if r == 0:
                push = push - forcing_at(n, l)
            hist[r, n + 1, 2, l] = rates[2, l] * hist[r, n, 2, l] + rates[5, l] * push

    def electric_first(r, n):
        hist[r, n + 1, 1, 0] = send_l[r, n, 0] + rates[4, 0] * (0.5 * recv_r[r, n, 1])
        hist[r, n + 1, 2, 0] = send_l[r, n, 1] - rates[5, 0] * (0.5 * recv_r[r, n, 0])

    def magnetic_at(r, n, l, ey_right, ez_right):
        ex, ey, ez = hist[r, n + 1, 0, l], hist[r, n + 1, 1, l], hist[r, n + 1, 2, l]
        mag[r, 0, l] = mag[r, 0, l] - 0.5 * (lead_j(ez) - ez - (lead_k(ey) - ey))
        mag[r, 1, l] = mag[r, 1, l] - 0.5 * (lead_k(ex) - ex - (ez_right - ez))
        mag[r, 2, l] = mag[r, 2, l] - 0.5 * (ey_right - ey - (lead_j(ex) - ex))

    def magnetic_last(r, n):
        ey = recv_l[r, n, 0] + ghost[0] * mag[r, 2, last]
        ez = recv_l[r, n, 1] - ghost[1] * mag[r, 1, last]
        magnetic_at(r, n, last, ey, ez)

    def magnetic_inner(r, n, l):
        magnetic_at(r, n, l, hist[r, n + 1, 1, l + 1], hist[r, n + 1, 2, l + 1])

    for r in range(2):
        make_edge(r, 0)
        start_edge(r, 0)

    def green_layer(w, carry):
        at = monitor - reach + w
        ok = (at >= 0) & (at < layers)
        place = jnp.clip(at, 0, layers - 1)
        label = labs[lax.div(place, width), lax.rem(place, width)]
        for c in range(3):
            keep, gain = rates_of(c, label)
            keep = jnp.where(ok, keep, 0.0)
            gain = jnp.where(ok, gain, 0.0)

            def put(b, v, c=c):
                green_rates[c, w, pl.ds(b * 8, 8)] = v

            def put_gain(b, v, c=c):
                green_rates[3 + c, w, pl.ds(b * 8, 8)] = v

            spread(put, keep)
            spread(put_gain, gain)
        return carry

    lax.fori_loop(0, 2 * reach + 1, green_layer, 0)
    green[0, 1, reach + 1] = -(green_rates[4, reach] * mon_ref[...])

    def green_magnetic(k):
        def one(w, carry):
            at = monitor - reach + w - 1
            half = jnp.where((at >= 0) & (at < layers), 0.5, 0.0)
            ex, ey, ez = green[k, 0, w], green[k, 1, w], green[k, 2, w]
            green_h[0, w] = green_h[0, w] - half * (lead_j(ez) - ez - (lead_k(ey) - ey))
            green_h[1, w] = green_h[1, w] - half * (lead_k(ex) - ex - (green[k, 2, w + 1] - ez))
            green_h[2, w] = green_h[2, w] - half * (green[k, 1, w + 1] - ey - (lead_j(ex) - ex))
            return carry

        lax.fori_loop(reach - k, reach + 2 + k, one, 0)

    def green_electric(k):
        def one(w, carry):
            hx, hy, hz = green_h[0, w], green_h[1, w], green_h[2, w]
            green[k, 0, w] = green_rates[0, w - 1] * green[k - 1, 0, w] + green_rates[3, w - 1] * (
                0.5 * (hz - lag_j(hz) - (hy - lag_k(hy)))
            )
            green[k, 1, w] = green_rates[1, w - 1] * green[k - 1, 1, w] + green_rates[4, w - 1] * (
                0.5 * (hx - lag_k(hx) - (hz - green_h[2, w - 1]))
            )
            green[k, 2, w] = green_rates[2, w - 1] * green[k - 1, 2, w] + green_rates[5, w - 1] * (
                0.5 * (hy - green_h[1, w - 1] - (hx - lag_j(hx)))
            )
            return carry

        lax.fori_loop(reach + 1 - k, reach + 2 + k, one, 0)

    def step(n, carry):
        for r in range(2):
            electric_inner(r, n)
        green_magnetic(n)
        green_electric(n + 1)
        for r in range(2):
            wait_right(r, n)
            electric_first(r, n)
            wait_left(r, n)
            magnetic_last(r, n)
            magnetic_inner(r, n, 0)
            make_edge(r, n + 1)
            start_edge(r, n + 1)
        for r in range(2):
            for l in range(1, last):
                magnetic_inner(r, n, l)
        return carry

    lax.fori_loop(0, STEPS - 1, step, 0)
    n = STEPS - 1
    for r in range(2):
        electric_inner(r, n)
    for r in range(2):
        wait_right(r, n)
        electric_first(r, n)

    mon_at = monitor - me * width
    mon_ok = jnp.where((mon_at >= 0) & (mon_at < width), 1.0, 0.0)
    mon_at = jnp.clip(mon_at, 0, width - 1)
    src_at = source - me * width
    src_ok = jnp.where((src_at >= 0) & (src_at < width), 1.0 / (rows * lanes), 0.0)
    src_at = jnp.clip(src_at, 0, width - 1)
    for t in range(STEPS):
        prod = hist[0, t + 1, 1, mon_at] * mon_ref[...]
        mid_own[t : t + 1] = jnp.sum(prod, axis=0, keepdims=True) * mon_ok
    for f in range(NF):
        re = jnp.zeros((rows, lanes), jnp.float32)
        im = jnp.zeros((rows, lanes), jnp.float32)
        for t in range(STEPS):
            field = hist[0, t + 1, 2, src_at]
            re = re + coef_ref[4 + f, t] * field
            im = im - coef_ref[8 + f, t] * field
        mid_own[STEPS + f : STEPS + f + 1] = (
            jnp.sum(re * re + im * im, axis=0, keepdims=True) * src_ok
        )
    mid_own[STEPS + NF :] = jnp.zeros((16 - STEPS - NF, lanes), jnp.float32)
    mid_begin()
    mids[me] = mid_own[...]
    mid_end()

    def add_mid(s, acc):
        return acc + mids[s]

    total = lax.fori_loop(1, nd, add_mid, mids[0])
    total = jnp.broadcast_to(jnp.sum(total, axis=1, keepdims=True), (16, lanes))
    root = 1.0 / math.sqrt(rows * lanes)
    amp = []
    for f in range(NF):
        scale = root / jnp.sqrt(total[STEPS + f : STEPS + f + 1] + 1e-06)
        re = jnp.zeros((1, lanes), jnp.float32)
        im = jnp.zeros((1, lanes), jnp.float32)
        for t in range(STEPS):
            re = re + coef_ref[4 + f, t] * total[t : t + 1]
            im = im - coef_ref[8 + f, t] * total[t : t + 1]
        amp.append((re * scale, im * scale))
    drive = []
    for t in range(STEPS):
        s = jnp.zeros((1, lanes), jnp.float32)
        for f in range(NF):
            s = s + amp[f][0] * coef_ref[4 + f, t] + amp[f][1] * coef_ref[8 + f, t]
        drive.append(jnp.broadcast_to(s, (8, lanes)))

    for l in range(width):
        w = me * width + l - monitor + reach + 1
        w = jnp.where((w >= 1) & (w <= 2 * reach + 1), w, 0)

        def correlate(i, carry, l=l, w=w):
            c = lax.div(i, blocks)
            b = lax.rem(i, blocks)
            at = pl.ds(pl.multiple_of(b * 8, 8), 8)
            first = [hist[0, t + 1, c, l, at] for t in range(STEPS)]
            impulse = [green[t, c, w, at] for t in range(STEPS)]
            second = []
            for t in range(STEPS):
                a = hist[1, t + 1, c, l, at]
                for m in range(t + 1):
                    a = a + drive[m] * impulse[t - m]
                second.append(a)
            perm = jnp.zeros((8, lanes), jnp.float32)
            cond = jnp.zeros((8, lanes), jnp.float32)
            for p in range(2 * STEPS - 1):
                q = None
                for t in range(max(0, p - STEPS + 1), min(p, STEPS - 1) + 1):
                    term = first[t] * second[p - t]
                    q = term if q is None else q + term
                perm = perm + coef_ref[0, p] * q
                cond = cond + coef_ref[1, p] * q
            cells[c, l, pl.ds(b, 1)] = jnp.sum(perm, axis=0, keepdims=True)
            cells[3 + c, l, pl.ds(b, 1)] = jnp.sum(cond, axis=0, keepdims=True)
            return carry

        lax.fori_loop(0, 3 * blocks, correlate, 0)

    left = lax.broadcasted_iota(jnp.int32, (lanes, lanes), 0)
    up = lax.broadcasted_iota(jnp.int32, (lanes, lanes), 1)
    pool = (lax.div(left, 8) == lax.div(up, 8)).astype(jnp.float32)
    flat = cells[...].reshape(6 * width * blocks, lanes)
    pooled = jnp.dot(flat, pool, precision=HIGH, preferred_element_type=jnp.float32)
    pooled = pooled.reshape(6 * width, blocks, lanes)
    sub = lax.broadcasted_iota(jnp.int32, (blocks, lanes), 0)
    lane = lax.broadcasted_iota(jnp.int32, (blocks, lanes), 1)
    mine = lax.rem(lane, 8) == sub
    packed = jnp.sum(jnp.where(mine[None], pooled, 0.0), axis=1).reshape(6, width, lanes)
    region = lax.broadcasted_iota(jnp.int32, (regions, lanes), 0)
    partial = jnp.zeros((8, regions), jnp.float32)
    for l in range(width):
        hot = (region == jnp.broadcast_to(packed_ref[l : l + 1], (regions, lanes))).astype(
            jnp.float32
        )
        these = jnp.concatenate([packed[:, l], jnp.zeros((2, lanes), jnp.float32)], axis=0)
        partial = partial + lax.dot_general(
            these, hot, (((1,), (1,)), ((), ())), precision=HIGH, preferred_element_type=jnp.float32
        )
    end_own[...] = partial * math.sqrt(regions / (layers * rows * lanes))
    end_begin()
    ends[me] = end_own[...]
    end_end()

    def add_end(s, acc):
        return acc + ends[s]

    summed = lax.fori_loop(1, nd, add_end, ends[0])
    chosen = lax.broadcasted_iota(jnp.int32, (regions, lanes), 0)
    wanted = lax.broadcasted_iota(jnp.int32, (regions, lanes), 1) + me * per
    pick = ((chosen == wanted) & (wanted < (me + 1) * per)).astype(jnp.float32)
    out_ref[...] = jnp.dot(summed, pick, precision=HIGH, preferred_element_type=jnp.float32)

    for r in range(2):

        def done(n, carry, r=r):
            @pl.when(me < nd - 1)
            def _():
                right_copy(r, n).wait_send()

            @pl.when((me > 0) & (n < STEPS - 1))
            def _():
                left_copy(r, n).wait_send()

            return carry

        lax.fori_loop(0, STEPS, done, 0)


def local(nd, e, h, ae, ah, perm, cond, labels, source, monitor, wave, src_mode, mon_mode):
    width, blocks = labels.shape[0], labels.shape[1]
    rows, lanes = src_mode.shape
    per = perm.shape[1]
    regions = nd * per
    me = lax.axis_index("domain")
    both = jnp.concatenate([perm, cond, jnp.zeros((2, per), jnp.float32)], 0)
    own = lax.div(jnp.arange(regions, dtype=jnp.int32), per) == me
    tab = jnp.where(own[None], jnp.tile(both, (1, nd)), 0.0)
    lab = jnp.repeat(labels, 8, axis=2)
    packed = jnp.transpose(labels, (0, 2, 1)).reshape(width, lanes)
    packed = jnp.concatenate([packed, jnp.zeros((-width % 8, lanes), jnp.int32)], 0)
    omega = 0.25 + 0.05 * wave.astype(jnp.float32)
    sums = jnp.arange(2, 2 * STEPS + 2).astype(jnp.float32)
    angle = omega[:, None] * sums[None]
    times = omega[:, None] * (jnp.arange(16).astype(jnp.float32) + 1.0)[None]
    coef = jnp.concatenate(
        [
            jnp.sum((omega * omega)[:, None] * jnp.cos(angle), axis=0)[None],
            -jnp.sum(omega[:, None] * jnp.sin(angle), axis=0)[None],
            jnp.sum(jnp.sin(times), axis=0)[None],
            jnp.zeros((1, 16), jnp.float32),
            jnp.cos(times),
            jnp.sin(times),
        ],
        0,
    )
    planes = jnp.concatenate([source, monitor])
    f32 = jnp.float32
    span = 2 * (STEPS - 1) + 1
    smem = pl.BlockSpec(memory_space=pltpu.SMEM)
    vmem = pl.BlockSpec(memory_space=pltpu.VMEM)
    hbm = pl.BlockSpec(memory_space=pl.ANY)
    dma = pltpu.SemaphoreType.DMA
    edge = pltpu.VMEM((2, STEPS, 2, rows, lanes), f32)
    out = pl.pallas_call(
        functools.partial(kernel, nd),
        out_shape=jax.ShapeDtypeStruct((8, lanes), f32),
        in_specs=[smem, smem, hbm, hbm, hbm, hbm, vmem, vmem, vmem, vmem, vmem],
        out_specs=vmem,
        scratch_shapes=[
            pltpu.VMEM((2, STEPS + 1, 3, width, rows, lanes), f32),
            pltpu.VMEM((2, 3, width, rows, lanes), f32),
            edge,
            edge,
            edge,
            edge,
            pltpu.VMEM((6, width, rows, lanes), f32),
            pltpu.VMEM((2, rows, lanes), f32),
            pltpu.VMEM((STEPS, 3, span + 2, rows, lanes), f32),
            pltpu.VMEM((3, span + 2, rows, lanes), f32),
            pltpu.VMEM((6, span, rows, lanes), f32),
            pltpu.VMEM((nd, 8, regions), f32),
            pltpu.VMEM((nd, width, blocks, lanes), jnp.int32),
            pltpu.VMEM((nd, 16, lanes), f32),
            pltpu.VMEM((nd, 8, regions), f32),
            pltpu.VMEM((6, width, blocks, lanes), f32),
            pltpu.VMEM((8, regions), f32),
            pltpu.VMEM((16, lanes), f32),
            pltpu.VMEM((8, regions), f32),
            dma((4,)),
            dma((2, STEPS)),
            dma((2, STEPS)),
            dma((2, STEPS)),
            dma((2, STEPS)),
            dma((4, nd)),
            dma((4, nd)),
        ],
        compiler_params=pltpu.CompilerParams(
            collective_id=0, has_side_effects=True, vmem_limit_bytes=60 * 1024 * 1024
        ),
    )(planes, coef, e, h, ae, ah, tab, lab, packed, src_mode, mon_mode)
    return out[:6, :per]


def solution(mesh):
    placed = (
        P(None, ("design", "domain"), None, None),
        P(None, ("design", "domain"), None, None),
        P(None, ("design", "domain"), None, None),
        P(None, ("design", "domain"), None, None),
        P(None, ("design", "domain")),
        P(None, ("design", "domain")),
        P(("design", "domain"), None, None),
        P("design"),
        P("design"),
        P("design"),
        P("design", None),
        P("design", None),
    )
    return jax.shard_map(
        functools.partial(local, mesh.shape["domain"]),
        mesh=mesh,
        in_specs=placed,
        out_specs=P(None, ("design", "domain")),
        check_vma=False,
    )
```

```python
import functools
import math

import jax
import jax.numpy as jnp
from jax import lax
from jax.experimental import pallas as pl
from jax.experimental.pallas import tpu as pltpu
from jax.sharding import PartitionSpec as P

STEPS = 8
NF = 4
MESH = pl.DeviceIdType.MESH
HIGH = lax.Precision.HIGHEST


def kernel(
    nd,
    source_ref,
    monitor_ref,
    wave_ref,
    e_hbm,
    h_hbm,
    ae_hbm,
    ah_hbm,
    perm_ref,
    cond_ref,
    lab_ref,
    src_ref,
    mon_ref,
    out_ref,
    hist,
    mag,
    send_r,
    send_l,
    recv_r,
    recv_l,
    rates,
    ghost,
    green,
    green_h,
    green_rates,
    facts,
    mids,
    ends,
    cells,
    tab_all,
    fact_own,
    wide,
    cos_t,
    sin_t,
    corr,
    mid_own,
    end_own,
    load_sem,
    sr_sem,
    sl_sem,
    rr_sem,
    rl_sem,
    g_send,
    g_recv,
):
    width = lab_ref.shape[0]
    rows, lanes = src_ref.shape
    blocks = rows // 8
    per = perm_ref.shape[1]
    regions = nd * per
    layers = nd * width
    me = lax.axis_index("domain")
    last = width - 1
    reach = STEPS - 1
    source = source_ref[0]
    monitor = monitor_ref[0]

    loads = []
    for r, (e, h) in enumerate(((e_hbm, h_hbm), (ae_hbm, ah_hbm))):
        loads.append(pltpu.make_async_copy(e, hist.at[r, 0], load_sem.at[2 * r]))
        loads.append(pltpu.make_async_copy(h, mag.at[r], load_sem.at[2 * r + 1]))
    for load in loads:
        load.start()

    barrier = pltpu.get_barrier_semaphore()

    def greet(j, carry):
        pl.semaphore_signal(
            barrier, inc=1, device_id={"domain": lax.rem(me + j, nd)}, device_id_type=MESH
        )
        return carry

    lax.fori_loop(1, nd, greet, 0)

    def to_all(phase, own, slots):
        def copy(j, away):
            return pltpu.make_async_remote_copy(
                src_ref=own,
                dst_ref=slots.at[away],
                send_sem=g_send.at[phase, j],
                recv_sem=g_recv.at[phase, j],
                device_id={"domain": lax.rem(me + j, nd)},
                device_id_type=MESH,
            )

        def begin():
            def one(j, carry):
                copy(j, me).start()
                return carry

            lax.fori_loop(1, nd, one, 0)

        def end():
            def one(j, carry):
                copy(j, me).wait_send()
                copy(j, lax.rem(me + nd - j, nd)).wait_recv()
                return carry

            lax.fori_loop(1, nd, one, 0)

        return begin, end

    fact_begin, fact_end = to_all(0, fact_own, facts)
    mid_begin, mid_end = to_all(1, mid_own, mids)
    end_begin, end_end = to_all(2, end_own, ends)

    tile_row = lax.broadcasted_iota(jnp.int32, (8, lanes), 0)
    tile_lane = lax.broadcasted_iota(jnp.int32, (8, lanes), 1)
    group = lax.div(tile_lane, 8)
    in_group = lax.rem(tile_lane, 8)
    by_lane = in_group == tile_row

    def flattened(x, mask):
        return jnp.sum(jnp.where(mask, x, 0.0), axis=0, keepdims=True)

    wide[...] = jnp.zeros_like(wide)
    wide[0, 0:3, 0:per] = perm_ref[...]
    wide[0, 3:6, 0:per] = cond_ref[...]
    for l in range(width):
        wide[1 + l, 0:blocks, 0 : lab_ref.shape[2]] = lab_ref[l].astype(jnp.float32)
    fact_own[...] = jnp.zeros_like(fact_own)
    repeated = jnp.take_along_axis(wide[0], lax.rem(tile_lane, per), axis=1)
    fact_own[0:1] = flattened(repeated, lax.div(tile_lane, per) == tile_row)
    for l in range(width):
        fact_own[1 + l : 2 + l] = flattened(
            jnp.take_along_axis(wide[1 + l], group, axis=1), by_lane
        )

    pl.semaphore_wait(barrier, nd - 1)
    fact_begin()
    facts[me] = fact_own[...]

    moment = (lax.broadcasted_iota(jnp.int32, (16, lanes), 0) + 1).astype(jnp.float32)
    weigh_perm = jnp.zeros((16, lanes), jnp.float32)
    weigh_cond = jnp.zeros((16, lanes), jnp.float32)
    drive_fwd = jnp.zeros((16, lanes), jnp.float32)
    for f in range(NF):
        omega = 0.25 + 0.05 * wave_ref[f].astype(jnp.float32)
        cosine = jnp.cos(moment * omega)
        sine = jnp.sin(moment * omega)
        cos_t[f] = cosine
        sin_t[f] = sine
        weigh_perm = weigh_perm + (omega * omega) * cosine
        weigh_cond = weigh_cond - omega * sine
        drive_fwd = drive_fwd + sine
    corr[0] = weigh_perm
    corr[1] = weigh_cond
    corr[2] = drive_fwd

    row_at = lax.broadcasted_iota(jnp.int32, (rows, lanes), 0)
    lane_at = lax.broadcasted_iota(jnp.int32, (rows, lanes), 1)

    def lag_j(x):
        return jnp.where(row_at == 0, 0.0, pltpu.roll(x, 1, 0))

    def lag_k(x):
        return jnp.where(lane_at == 0, 0.0, pltpu.roll(x, 1, 1))

    def lead_j(x):
        return jnp.where(row_at == rows - 1, 0.0, pltpu.roll(x, rows - 1, 0))

    def lead_k(x):
        return jnp.where(lane_at == lanes - 1, 0.0, pltpu.roll(x, lanes - 1, 1))

    @pl.when(me == 0)
    def _():
        recv_r[...] = jnp.zeros_like(recv_r)

    @pl.when(me == nd - 1)
    def _():
        recv_l[...] = jnp.zeros_like(recv_l)

    def clear(w, carry):
        zero = jnp.zeros((rows, lanes), jnp.float32)
        for k in range(STEPS):
            for c in range(3):
                green[k, c, w] = zero
        for c in range(3):
            green_h[c, w] = zero
        return carry

    lax.fori_loop(0, 2 * reach + 3, clear, 0)

    fact_end()

    each = lanes // per
    seat = lax.broadcasted_iota(jnp.int32, (each, lanes), 0)
    lane_of = lax.broadcasted_iota(jnp.int32, (each, lanes), 1)
    for q in range(regions // lanes):
        row = facts[q * each : (q + 1) * each, 0]
        for c in range(6):
            found = jnp.take_along_axis(row, c * per + lax.rem(lane_of, per), axis=1)
            tab_all[c : c + 1, q * lanes : (q + 1) * lanes] = flattened(
                found, lax.div(lane_of, per) == seat
            )

    def layer_labels(device, l):
        row = jnp.broadcast_to(facts[device, pl.ds(1 + l, 1)], (blocks, lanes))
        return jnp.take_along_axis(row, group * 8 + tile_row, axis=1).astype(jnp.int32)

    def looked_up(c, label):
        value = jnp.zeros(label.shape, jnp.float32)
        for q in range(regions // lanes):
            row = jnp.broadcast_to(tab_all[c : c + 1, q * lanes : (q + 1) * lanes], label.shape)
            found = jnp.take_along_axis(row, lax.rem(label, lanes), axis=1)
            value = jnp.where(lax.div(label, lanes) == q, found, value)
        return value

    def rates_of(c, label):
        perm = looked_up(c, label)
        cond = looked_up(3 + c, label)
        loss = cond * 0.5 / perm
        return (1.0 - loss) / (1.0 + loss), 1.0 / (perm * (1.0 + loss))

    def spread(write, value):
        for b in range(blocks):
            write(b, jnp.broadcast_to(value[b : b + 1], (8, lanes)))

    for l in range(width):
        label = layer_labels(me, l)
        for c in range(3):
            keep, gain = rates_of(c, label)

            def put(b, v, c=c, l=l):
                rates[c, l, pl.ds(b * 8, 8)] = v

            def put_gain(b, v, c=c, l=l):
                rates[3 + c, l, pl.ds(b * 8, 8)] = v

            spread(put, keep)
            spread(put_gain, gain)

    after = lax.rem(me + 1, nd)
    inside = jnp.where(me == nd - 1, 0.0, 0.5)
    label = layer_labels(after, 0)
    for c in (1, 2):
        _, gain = rates_of(c, label)

        def put_ghost(b, v, c=c):
            ghost[c - 1, pl.ds(b * 8, 8)] = v * inside

        spread(put_ghost, gain)

    for load in loads:
        load.wait()

    def forcing_at(n, l):
        lit = jnp.where(source == me * width + l, 1.0, 0.0)
        return src_ref[...] * (corr[2, pl.ds(n, 1)] * lit)

    def make_edge(r, n):
        for c in (1, 2):
            send_r[r, n, c - 1] = mag[r, c, last]
        hx, hy, hz = mag[r, 0, 0], mag[r, 1, 0], mag[r, 2, 0]
        py = rates[1, 0] * hist[r, n, 1, 0] + rates[4, 0] * (0.5 * (hx - lag_k(hx) - hz))
        push = 0.5 * (hy - (hx - lag_j(hx)))
        if r == 0:
            push = push - forcing_at(n, 0)
        pz = rates[2, 0] * hist[r, n, 2, 0] + rates[5, 0] * push
        send_l[r, n, 0] = py
        send_l[r, n, 1] = pz

    def right_copy(r, n):
        return pltpu.make_async_remote_copy(
            src_ref=send_r.at[r, n],
            dst_ref=recv_r.at[r, n],
            send_sem=sr_sem.at[r, n],
            recv_sem=rr_sem.at[r, n],
            device_id={"domain": lax.rem(me + 1, nd)},
            device_id_type=MESH,
        )

    def left_copy(r, n):
        return pltpu.make_async_remote_copy(
            src_ref=send_l.at[r, n],
            dst_ref=recv_l.at[r, n],
            send_sem=sl_sem.at[r, n],
            recv_sem=rl_sem.at[r, n],
            device_id={"domain": lax.rem(me + nd - 1, nd)},
            device_id_type=MESH,
        )

    def start_edge(r, n):
        @pl.when(me < nd - 1)
        def _():
            right_copy(r, n).start()

        @pl.when((me > 0) & (n < STEPS - 1))
        def _():
            left_copy(r, n).start()

    def wait_right(r, n):
        @pl.when(me > 0)
        def _():
            right_copy(r, n).wait_recv()

    def wait_left(r, n):
        @pl.when(me < nd - 1)
        def _():
            left_copy(r, n).wait_recv()

    def electric_inner(r, n):
        for l in range(width):
            hx, hy, hz = mag[r, 0, l], mag[r, 1, l], mag[r, 2, l]
            hist[r, n + 1, 0, l] = rates[0, l] * hist[r, n, 0, l] + rates[3, l] * (
                0.5 * (hz - lag_j(hz) - (hy - lag_k(hy)))
            )
            if l == 0:
                continue
            hist[r, n + 1, 1, l] = rates[1, l] * hist[r, n, 1, l] + rates[4, l] * (
                0.5 * (hx - lag_k(hx) - (hz - mag[r, 2, l - 1]))
            )
            push = 0.5 * (hy - mag[r, 1, l - 1] - (hx - lag_j(hx)))
            if r == 0:
                push = push - forcing_at(n, l)
            hist[r, n + 1, 2, l] = rates[2, l] * hist[r, n, 2, l] + rates[5, l] * push

    def electric_first(r, n):
        hist[r, n + 1, 1, 0] = send_l[r, n, 0] + rates[4, 0] * (0.5 * recv_r[r, n, 1])
        hist[r, n + 1, 2, 0] = send_l[r, n, 1] - rates[5, 0] * (0.5 * recv_r[r, n, 0])

    def magnetic_at(r, n, l, ey_right, ez_right):
        ex, ey, ez = hist[r, n + 1, 0, l], hist[r, n + 1, 1, l], hist[r, n + 1, 2, l]
        mag[r, 0, l] = mag[r, 0, l] - 0.5 * (lead_j(ez) - ez - (lead_k(ey) - ey))
        mag[r, 1, l] = mag[r, 1, l] - 0.5 * (lead_k(ex) - ex - (ez_right - ez))
        mag[r, 2, l] = mag[r, 2, l] - 0.5 * (ey_right - ey - (lead_j(ex) - ex))

    def magnetic_last(r, n):
        ey = recv_l[r, n, 0] + ghost[0] * mag[r, 2, last]
        ez = recv_l[r, n, 1] - ghost[1] * mag[r, 1, last]
        magnetic_at(r, n, last, ey, ez)

    def magnetic_inner(r, n, l):
        magnetic_at(r, n, l, hist[r, n + 1, 1, l + 1], hist[r, n + 1, 2, l + 1])

    for r in range(2):
        make_edge(r, 0)
        start_edge(r, 0)

    def green_layer(w, carry):
        at = monitor - reach + w
        ok = (at >= 0) & (at < layers)
        place = jnp.clip(at, 0, layers - 1)
        label = layer_labels(lax.div(place, width), lax.rem(place, width))
        for c in range(3):
            keep, gain = rates_of(c, label)
            keep = jnp.where(ok, keep, 0.0)
            gain = jnp.where(ok, gain, 0.0)

            def put(b, v, c=c):
                green_rates[c, w, pl.ds(b * 8, 8)] = v

            def put_gain(b, v, c=c):
                green_rates[3 + c, w, pl.ds(b * 8, 8)] = v

            spread(put, keep)
            spread(put_gain, gain)
        return carry

    lax.fori_loop(0, 2 * reach + 1, green_layer, 0)
    green[0, 1, reach + 1] = -(green_rates[4, reach] * mon_ref[...])

    def green_magnetic(k):
        def one(w, carry):
            at = monitor - reach + w - 1
            half = jnp.where((at >= 0) & (at < layers), 0.5, 0.0)
            ex, ey, ez = green[k, 0, w], green[k, 1, w], green[k, 2, w]
            green_h[0, w] = green_h[0, w] - half * (lead_j(ez) - ez - (lead_k(ey) - ey))
            green_h[1, w] = green_h[1, w] - half * (lead_k(ex) - ex - (green[k, 2, w + 1] - ez))
            green_h[2, w] = green_h[2, w] - half * (green[k, 1, w + 1] - ey - (lead_j(ex) - ex))
            return carry

        lax.fori_loop(reach - k, reach + 2 + k, one, 0)

    def green_electric(k):
        def one(w, carry):
            hx, hy, hz = green_h[0, w], green_h[1, w], green_h[2, w]
            green[k, 0, w] = green_rates[0, w - 1] * green[k - 1, 0, w] + green_rates[3, w - 1] * (
                0.5 * (hz - lag_j(hz) - (hy - lag_k(hy)))
            )
            green[k, 1, w] = green_rates[1, w - 1] * green[k - 1, 1, w] + green_rates[4, w - 1] * (
                0.5 * (hx - lag_k(hx) - (hz - green_h[2, w - 1]))
            )
            green[k, 2, w] = green_rates[2, w - 1] * green[k - 1, 2, w] + green_rates[5, w - 1] * (
                0.5 * (hy - green_h[1, w - 1] - (hx - lag_j(hx)))
            )
            return carry

        lax.fori_loop(reach + 1 - k, reach + 2 + k, one, 0)

    def step(n, carry):
        for r in range(2):
            electric_inner(r, n)
        green_magnetic(n)
        green_electric(n + 1)
        for r in range(2):
            wait_right(r, n)
            electric_first(r, n)
            wait_left(r, n)
            magnetic_last(r, n)
            magnetic_inner(r, n, 0)
            make_edge(r, n + 1)
            start_edge(r, n + 1)
        for r in range(2):
            for l in range(1, last):
                magnetic_inner(r, n, l)
        return carry

    lax.fori_loop(0, STEPS - 1, step, 0)
    n = STEPS - 1
    electric_inner(0, n)
    wait_right(0, n)
    electric_first(0, n)

    mon_at = monitor - me * width
    mon_ok = jnp.where((mon_at >= 0) & (mon_at < width), 1.0, 0.0)
    mon_at = jnp.clip(mon_at, 0, width - 1)
    src_at = source - me * width
    src_ok = jnp.where((src_at >= 0) & (src_at < width), 1.0 / (rows * lanes), 0.0)
    src_at = jnp.clip(src_at, 0, width - 1)
    for t in range(STEPS):
        prod = hist[0, t + 1, 1, mon_at] * mon_ref[...]
        mid_own[t : t + 1] = jnp.sum(prod, axis=0, keepdims=True) * mon_ok
    for f in range(NF):
        re = jnp.zeros((rows, lanes), jnp.float32)
        im = jnp.zeros((rows, lanes), jnp.float32)
        for t in range(STEPS):
            field = hist[0, t + 1, 2, src_at]
            re = re + cos_t[f, t : t + 1] * field
            im = im - sin_t[f, t : t + 1] * field
        mid_own[STEPS + f : STEPS + f + 1] = (
            jnp.sum(re * re + im * im, axis=0, keepdims=True) * src_ok
        )
    mid_own[STEPS + NF :] = jnp.zeros((16 - STEPS - NF, lanes), jnp.float32)
    mid_begin()
    mids[me] = mid_own[...]
    electric_inner(1, n)
    wait_right(1, n)
    electric_first(1, n)
    mid_end()

    def add_mid(s, acc):
        return acc + mids[s]

    total = lax.fori_loop(1, nd, add_mid, mids[0])
    total = jnp.broadcast_to(jnp.sum(total, axis=1, keepdims=True), (16, lanes))
    root = 1.0 / math.sqrt(rows * lanes)
    amp = []
    for f in range(NF):
        scale = root / jnp.sqrt(total[STEPS + f : STEPS + f + 1] + 1e-06)
        re = jnp.zeros((1, lanes), jnp.float32)
        im = jnp.zeros((1, lanes), jnp.float32)
        for t in range(STEPS):
            re = re + cos_t[f, t : t + 1] * total[t : t + 1]
            im = im - sin_t[f, t : t + 1] * total[t : t + 1]
        amp.append((re * scale, im * scale))
    drive = []
    for t in range(STEPS):
        s = jnp.zeros((1, lanes), jnp.float32)
        for f in range(NF):
            s = s + amp[f][0] * cos_t[f, t : t + 1] + amp[f][1] * sin_t[f, t : t + 1]
        drive.append(jnp.broadcast_to(s, (8, lanes)))

    for l in range(width):
        w = me * width + l - monitor + reach + 1
        w = jnp.where((w >= 1) & (w <= 2 * reach + 1), w, 0)

        def correlate(i, carry, l=l, w=w):
            c = lax.div(i, blocks)
            b = lax.rem(i, blocks)
            at = pl.ds(pl.multiple_of(b * 8, 8), 8)
            first = [hist[0, t + 1, c, l, at] for t in range(STEPS)]
            impulse = [green[t, c, w, at] for t in range(STEPS)]
            second = []
            for t in range(STEPS):
                a = hist[1, t + 1, c, l, at]
                for m in range(t + 1):
                    a = a + drive[m] * impulse[t - m]
                second.append(a)
            perm = jnp.zeros((8, lanes), jnp.float32)
            cond = jnp.zeros((8, lanes), jnp.float32)
            for p in range(2 * STEPS - 1):
                q = None
                for t in range(max(0, p - STEPS + 1), min(p, STEPS - 1) + 1):
                    term = first[t] * second[p - t]
                    q = term if q is None else q + term
                perm = perm + corr[0, p + 1 : p + 2] * q
                cond = cond + corr[1, p + 1 : p + 2] * q
            cells[c, l, pl.ds(b, 1)] = jnp.sum(perm, axis=0, keepdims=True)
            cells[3 + c, l, pl.ds(b, 1)] = jnp.sum(cond, axis=0, keepdims=True)
            return carry

        lax.fori_loop(0, 3 * blocks, correlate, 0)

    left = lax.broadcasted_iota(jnp.int32, (lanes, lanes), 0)
    up = lax.broadcasted_iota(jnp.int32, (lanes, lanes), 1)
    pool = (lax.div(left, 8) == lax.div(up, 8)).astype(jnp.float32)
    flat = cells[...].reshape(6 * width * blocks, lanes)
    pooled = jnp.dot(flat, pool, precision=HIGH, preferred_element_type=jnp.float32)
    pooled = pooled.reshape(6 * width, blocks, lanes)
    sub = lax.broadcasted_iota(jnp.int32, (blocks, lanes), 0)
    lane = lax.broadcasted_iota(jnp.int32, (blocks, lanes), 1)
    mine = lax.rem(lane, 8) == sub
    packed = jnp.sum(jnp.where(mine[None], pooled, 0.0), axis=1).reshape(6, width, lanes)
    region = lax.broadcasted_iota(jnp.int32, (regions, lanes), 0)
    partial = jnp.zeros((8, regions), jnp.float32)
    for l in range(width):
        hot = (region == jnp.broadcast_to(
                fact_own[1 + l : 2 + l].astype(jnp.int32), (regions, lanes)
            )).astype(
            jnp.float32
        )
        these = jnp.concatenate([packed[:, l], jnp.zeros((2, lanes), jnp.float32)], axis=0)
        partial = partial + lax.dot_general(
            these, hot, (((1,), (1,)), ((), ())), precision=HIGH, preferred_element_type=jnp.float32
        )
    end_own[...] = partial * math.sqrt(regions / (layers * rows * lanes))
    end_begin()
    ends[me] = end_own[...]
    end_end()

    def add_end(s, acc):
        return acc + ends[s]

    summed = lax.fori_loop(1, nd, add_end, ends[0])
    chosen = lax.broadcasted_iota(jnp.int32, (regions, lanes), 0)
    wanted = lax.broadcasted_iota(jnp.int32, (regions, lanes), 1) + me * per
    pick = ((chosen == wanted) & (wanted < (me + 1) * per)).astype(jnp.float32)
    mine = jnp.dot(summed, pick, precision=HIGH, preferred_element_type=jnp.float32)
    out_ref[...] = mine[:6, :per]

    for r in range(2):

        def done(n, carry, r=r):
            @pl.when(me < nd - 1)
            def _():
                right_copy(r, n).wait_send()

            @pl.when((me > 0) & (n < STEPS - 1))
            def _():
                left_copy(r, n).wait_send()

            return carry

        lax.fori_loop(0, STEPS, done, 0)


def local(nd, e, h, ae, ah, perm, cond, labels, source, monitor, wave, src_mode, mon_mode):
    width, blocks = labels.shape[0], labels.shape[1]
    rows, lanes = src_mode.shape
    per = perm.shape[1]
    regions = nd * per
    f32 = jnp.float32
    span = 2 * (STEPS - 1) + 1
    smem = pl.BlockSpec(memory_space=pltpu.SMEM)
    vmem = pl.BlockSpec(memory_space=pltpu.VMEM)
    hbm = pl.BlockSpec(memory_space=pl.ANY)
    dma = pltpu.SemaphoreType.DMA
    edge = pltpu.VMEM((2, STEPS, 2, rows, lanes), f32)
    out = pl.pallas_call(
        functools.partial(kernel, nd),
        out_shape=jax.ShapeDtypeStruct((6, per), f32),
        in_specs=[smem, smem, smem, hbm, hbm, hbm, hbm, vmem, vmem, vmem, vmem, vmem],
        out_specs=vmem,
        scratch_shapes=[
            pltpu.VMEM((2, STEPS + 1, 3, width, rows, lanes), f32),
            pltpu.VMEM((2, 3, width, rows, lanes), f32),
            edge,
            edge,
            edge,
            edge,
            pltpu.VMEM((6, width, rows, lanes), f32),
            pltpu.VMEM((2, rows, lanes), f32),
            pltpu.VMEM((STEPS, 3, span + 2, rows, lanes), f32),
            pltpu.VMEM((3, span + 2, rows, lanes), f32),
            pltpu.VMEM((6, span, rows, lanes), f32),
            pltpu.VMEM((nd, 8, lanes), f32),
            pltpu.VMEM((nd, 16, lanes), f32),
            pltpu.VMEM((nd, 8, regions), f32),
            pltpu.VMEM((6, width, blocks, lanes), f32),
            pltpu.VMEM((8, regions), f32),
            pltpu.VMEM((8, lanes), f32),
            pltpu.VMEM((1 + width, 8, lanes), f32),
            pltpu.VMEM((NF, 16, lanes), f32),
            pltpu.VMEM((NF, 16, lanes), f32),
            pltpu.VMEM((3, 16, lanes), f32),
            pltpu.VMEM((16, lanes), f32),
            pltpu.VMEM((8, regions), f32),
            dma((4,)),
            dma((2, STEPS)),
            dma((2, STEPS)),
            dma((2, STEPS)),
            dma((2, STEPS)),
            dma((3, nd)),
            dma((3, nd)),
        ],
        compiler_params=pltpu.CompilerParams(
            collective_id=0, has_side_effects=True, vmem_limit_bytes=60 * 1024 * 1024
        ),
    )(source, monitor, wave, e, h, ae, ah, perm, cond, labels, src_mode, mon_mode)
    return out


def solution(mesh):
    placed = (
        P(None, ("design", "domain"), None, None),
        P(None, ("design", "domain"), None, None),
        P(None, ("design", "domain"), None, None),
        P(None, ("design", "domain"), None, None),
        P(None, ("design", "domain")),
        P(None, ("design", "domain")),
        P(("design", "domain"), None, None),
        P("design"),
        P("design"),
        P("design"),
        P("design", None),
        P("design", None),
    )
    return jax.shard_map(
        functools.partial(local, mesh.shape["domain"]),
        mesh=mesh,
        in_specs=placed,
        out_specs=P(None, ("design", "domain")),
        check_vma=False,
    )
```

```python
import functools
import math

import jax
import jax.numpy as jnp
from jax import lax
from jax.experimental import pallas as pl
from jax.experimental.pallas import tpu as pltpu
from jax.sharding import PartitionSpec as P

STEPS = 8
NF = 4
MESH = pl.DeviceIdType.MESH
HIGH = lax.Precision.HIGHEST


def kernel(
    nd,
    source_ref,
    monitor_ref,
    wave_ref,
    e_hbm,
    h_hbm,
    ae_hbm,
    ah_hbm,
    perm_ref,
    cond_ref,
    lab_ref,
    src_ref,
    mon_ref,
    out_ref,
    hist,
    mag,
    send_r,
    send_l,
    recv_r,
    recv_l,
    rates,
    ghost,
    green,
    green_h,
    green_rates,
    facts,
    mids,
    ends,
    cells,
    tab_all,
    fact_own,
    wide,
    cos_t,
    sin_t,
    corr,
    mid_own,
    end_own,
    load_sem,
    sr_sem,
    sl_sem,
    rr_sem,
    rl_sem,
    g_send,
    g_recv,
):
    width = lab_ref.shape[0]
    rows, lanes = src_ref.shape
    blocks = rows // 8
    per = perm_ref.shape[1]
    regions = nd * per
    layers = nd * width
    me = lax.axis_index("domain")
    last = width - 1
    reach = STEPS - 1
    source = source_ref[0]
    monitor = monitor_ref[0]

    loads = []
    for r, (e, h) in enumerate(((e_hbm, h_hbm), (ae_hbm, ah_hbm))):
        loads.append(pltpu.make_async_copy(e, hist.at[r, 0], load_sem.at[2 * r]))
        loads.append(pltpu.make_async_copy(h, mag.at[r], load_sem.at[2 * r + 1]))
    for load in loads:
        load.start()

    barrier = pltpu.get_barrier_semaphore()

    def greet(j, carry):
        pl.semaphore_signal(
            barrier, inc=1, device_id={"domain": lax.rem(me + j, nd)}, device_id_type=MESH
        )
        return carry

    lax.fori_loop(1, nd, greet, 0)

    def to_all(phase, own, slots):
        def copy(j, away):
            return pltpu.make_async_remote_copy(
                src_ref=own,
                dst_ref=slots.at[away],
                send_sem=g_send.at[phase, j],
                recv_sem=g_recv.at[phase, j],
                device_id={"domain": lax.rem(me + j, nd)},
                device_id_type=MESH,
            )

        def begin():
            def one(j, carry):
                copy(j, me).start()
                return carry

            lax.fori_loop(1, nd, one, 0)

        def end():
            def one(j, carry):
                copy(j, me).wait_send()
                copy(j, lax.rem(me + nd - j, nd)).wait_recv()
                return carry

            lax.fori_loop(1, nd, one, 0)

        return begin, end

    fact_begin, fact_end = to_all(0, fact_own, facts)
    mid_begin, mid_end = to_all(1, mid_own, mids)
    end_begin, end_end = to_all(2, end_own, ends)

    tile_row = lax.broadcasted_iota(jnp.int32, (8, lanes), 0)
    tile_lane = lax.broadcasted_iota(jnp.int32, (8, lanes), 1)
    group = lax.div(tile_lane, 8)
    in_group = lax.rem(tile_lane, 8)
    by_lane = in_group == tile_row

    def flattened(x, mask):
        return jnp.sum(jnp.where(mask, x, 0.0), axis=0, keepdims=True)

    wide[...] = jnp.zeros_like(wide)
    wide[0, 0:3, 0:per] = perm_ref[...]
    wide[0, 3:6, 0:per] = cond_ref[...]
    for l in range(width):
        wide[1 + l, 0:blocks, 0 : lab_ref.shape[2]] = lab_ref[l].astype(jnp.float32)
    fact_own[...] = jnp.zeros_like(fact_own)
    repeated = jnp.take_along_axis(wide[0], lax.rem(tile_lane, per), axis=1)
    fact_own[0:1] = flattened(repeated, lax.div(tile_lane, per) == tile_row)
    for l in range(width):
        fact_own[1 + l : 2 + l] = flattened(
            jnp.take_along_axis(wide[1 + l], group, axis=1), by_lane
        )

    pl.semaphore_wait(barrier, nd - 1)
    fact_begin()
    facts[me] = fact_own[...]

    moment = (lax.broadcasted_iota(jnp.int32, (16, lanes), 0) + 1).astype(jnp.float32)
    weigh_perm = jnp.zeros((16, lanes), jnp.float32)
    weigh_cond = jnp.zeros((16, lanes), jnp.float32)
    drive_fwd = jnp.zeros((16, lanes), jnp.float32)
    for f in range(NF):
        omega = 0.25 + 0.05 * wave_ref[f].astype(jnp.float32)
        cosine = jnp.cos(moment * omega)
        sine = jnp.sin(moment * omega)
        cos_t[f] = cosine
        sin_t[f] = sine
        weigh_perm = weigh_perm + (omega * omega) * cosine
        weigh_cond = weigh_cond - omega * sine
        drive_fwd = drive_fwd + sine
    corr[0] = weigh_perm
    corr[1] = weigh_cond
    corr[2] = drive_fwd

    row_at = lax.broadcasted_iota(jnp.int32, (rows, lanes), 0)
    lane_at = lax.broadcasted_iota(jnp.int32, (rows, lanes), 1)

    def lag_j(x):
        return jnp.where(row_at == 0, 0.0, pltpu.roll(x, 1, 0))

    def lag_k(x):
        return jnp.where(lane_at == 0, 0.0, pltpu.roll(x, 1, 1))

    def lead_j(x):
        return jnp.where(row_at == rows - 1, 0.0, pltpu.roll(x, rows - 1, 0))

    def lead_k(x):
        return jnp.where(lane_at == lanes - 1, 0.0, pltpu.roll(x, lanes - 1, 1))

    @pl.when(me == 0)
    def _():
        recv_r[...] = jnp.zeros_like(recv_r)

    @pl.when(me == nd - 1)
    def _():
        recv_l[...] = jnp.zeros_like(recv_l)

    def clear(w, carry):
        zero = jnp.zeros((rows, lanes), jnp.float32)
        for k in range(STEPS):
            for c in range(3):
                green[k, c, w] = zero
        for c in range(3):
            green_h[c, w] = zero
        return carry

    lax.fori_loop(0, 2 * reach + 3, clear, 0)

    fact_end()

    each = lanes // per
    seat = lax.broadcasted_iota(jnp.int32, (each, lanes), 0)
    lane_of = lax.broadcasted_iota(jnp.int32, (each, lanes), 1)
    for q in range(regions // lanes):
        row = facts[q * each : (q + 1) * each, 0]
        for c in range(6):
            found = jnp.take_along_axis(row, c * per + lax.rem(lane_of, per), axis=1)
            tab_all[c : c + 1, q * lanes : (q + 1) * lanes] = flattened(
                found, lax.div(lane_of, per) == seat
            )

    def layer_labels(device, l):
        row = jnp.broadcast_to(facts[device, pl.ds(1 + l, 1)], (blocks, lanes))
        return jnp.take_along_axis(row, group * 8 + tile_row, axis=1).astype(jnp.int32)

    def looked_up(c, label):
        value = jnp.zeros(label.shape, jnp.float32)
        for q in range(regions // lanes):
            row = jnp.broadcast_to(tab_all[c : c + 1, q * lanes : (q + 1) * lanes], label.shape)
            found = jnp.take_along_axis(row, lax.rem(label, lanes), axis=1)
            value = jnp.where(lax.div(label, lanes) == q, found, value)
        return value

    def rates_of(c, label):
        perm = looked_up(c, label)
        cond = looked_up(3 + c, label)
        loss = cond * 0.5 / perm
        return (1.0 - loss) / (1.0 + loss), 1.0 / (perm * (1.0 + loss))

    def spread(write, value):
        for b in range(blocks):
            write(b, jnp.broadcast_to(value[b : b + 1], (8, lanes)))

    for l in range(width):
        label = layer_labels(me, l)
        for c in range(3):
            keep, gain = rates_of(c, label)

            def put(b, v, c=c, l=l):
                rates[c, l, pl.ds(b * 8, 8)] = v

            def put_gain(b, v, c=c, l=l):
                rates[3 + c, l, pl.ds(b * 8, 8)] = v

            spread(put, keep)
            spread(put_gain, gain)

    after = lax.rem(me + 1, nd)
    inside = jnp.where(me == nd - 1, 0.0, 0.5)
    label = layer_labels(after, 0)
    for c in (1, 2):
        _, gain = rates_of(c, label)

        def put_ghost(b, v, c=c):
            ghost[c - 1, pl.ds(b * 8, 8)] = v * inside

        spread(put_ghost, gain)

    for load in loads:
        load.wait()

    def forcing_at(n, l):
        lit = jnp.where(source == me * width + l, 1.0, 0.0)
        return src_ref[...] * (corr[2, pl.ds(n, 1)] * lit)

    def make_edge(r, n):
        for c in (1, 2):
            send_r[r, n, c - 1] = mag[r, c, last]
        hx, hy, hz = mag[r, 0, 0], mag[r, 1, 0], mag[r, 2, 0]
        py = rates[1, 0] * hist[r, n, 1, 0] + rates[4, 0] * (0.5 * (hx - lag_k(hx) - hz))
        push = 0.5 * (hy - (hx - lag_j(hx)))
        if r == 0:
            push = push - forcing_at(n, 0)
        pz = rates[2, 0] * hist[r, n, 2, 0] + rates[5, 0] * push
        send_l[r, n, 0] = py
        send_l[r, n, 1] = pz

    def right_copy(r, n):
        return pltpu.make_async_remote_copy(
            src_ref=send_r.at[r, n],
            dst_ref=recv_r.at[r, n],
            send_sem=sr_sem.at[r, n],
            recv_sem=rr_sem.at[r, n],
            device_id={"domain": lax.rem(me + 1, nd)},
            device_id_type=MESH,
        )

    def left_copy(r, n):
        return pltpu.make_async_remote_copy(
            src_ref=send_l.at[r, n],
            dst_ref=recv_l.at[r, n],
            send_sem=sl_sem.at[r, n],
            recv_sem=rl_sem.at[r, n],
            device_id={"domain": lax.rem(me + nd - 1, nd)},
            device_id_type=MESH,
        )

    def start_edge(r, n):
        @pl.when(me < nd - 1)
        def _():
            right_copy(r, n).start()

        @pl.when((me > 0) & (n < STEPS - 1))
        def _():
            left_copy(r, n).start()

    def wait_right(r, n):
        @pl.when(me > 0)
        def _():
            right_copy(r, n).wait_recv()

    def wait_left(r, n):
        @pl.when(me < nd - 1)
        def _():
            left_copy(r, n).wait_recv()

    def electric_inner(r, n):
        for l in range(width):
            hx, hy, hz = mag[r, 0, l], mag[r, 1, l], mag[r, 2, l]
            hist[r, n + 1, 0, l] = rates[0, l] * hist[r, n, 0, l] + rates[3, l] * (
                0.5 * (hz - lag_j(hz) - (hy - lag_k(hy)))
            )
            if l == 0:
                continue
            hist[r, n + 1, 1, l] = rates[1, l] * hist[r, n, 1, l] + rates[4, l] * (
                0.5 * (hx - lag_k(hx) - (hz - mag[r, 2, l - 1]))
            )
            push = 0.5 * (hy - mag[r, 1, l - 1] - (hx - lag_j(hx)))
            if r == 0:
                push = push - forcing_at(n, l)
            hist[r, n + 1, 2, l] = rates[2, l] * hist[r, n, 2, l] + rates[5, l] * push

    def electric_first(r, n):
        hist[r, n + 1, 1, 0] = send_l[r, n, 0] + rates[4, 0] * (0.5 * recv_r[r, n, 1])
        hist[r, n + 1, 2, 0] = send_l[r, n, 1] - rates[5, 0] * (0.5 * recv_r[r, n, 0])

    def magnetic_at(r, n, l, ey_right, ez_right):
        ex, ey, ez = hist[r, n + 1, 0, l], hist[r, n + 1, 1, l], hist[r, n + 1, 2, l]
        mag[r, 0, l] = mag[r, 0, l] - 0.5 * (lead_j(ez) - ez - (lead_k(ey) - ey))
        mag[r, 1, l] = mag[r, 1, l] - 0.5 * (lead_k(ex) - ex - (ez_right - ez))
        mag[r, 2, l] = mag[r, 2, l] - 0.5 * (ey_right - ey - (lead_j(ex) - ex))

    def magnetic_last(r, n):
        ey = recv_l[r, n, 0] + ghost[0] * mag[r, 2, last]
        ez = recv_l[r, n, 1] - ghost[1] * mag[r, 1, last]
        magnetic_at(r, n, last, ey, ez)

    def magnetic_inner(r, n, l):
        magnetic_at(r, n, l, hist[r, n + 1, 1, l + 1], hist[r, n + 1, 2, l + 1])

    for r in range(2):
        make_edge(r, 0)
        start_edge(r, 0)

    def green_layer(w, carry):
        at = monitor - reach + w
        ok = (at >= 0) & (at < layers)
        place = jnp.clip(at, 0, layers - 1)
        label = layer_labels(lax.div(place, width), lax.rem(place, width))
        for c in range(3):
            keep, gain = rates_of(c, label)
            keep = jnp.where(ok, keep, 0.0)
            gain = jnp.where(ok, gain, 0.0)

            def put(b, v, c=c):
                green_rates[c, w, pl.ds(b * 8, 8)] = v

            def put_gain(b, v, c=c):
                green_rates[3 + c, w, pl.ds(b * 8, 8)] = v

            spread(put, keep)
            spread(put_gain, gain)
        return carry

    lax.fori_loop(0, 2 * reach + 1, green_layer, 0)
    green[0, 1, reach + 1] = -(green_rates[4, reach] * mon_ref[...])

    def green_magnetic(k):
        def one(w, carry):
            at = monitor - reach + w - 1
            half = jnp.where((at >= 0) & (at < layers), 0.5, 0.0)
            ex, ey, ez = green[k, 0, w], green[k, 1, w], green[k, 2, w]
            green_h[0, w] = green_h[0, w] - half * (lead_j(ez) - ez - (lead_k(ey) - ey))
            green_h[1, w] = green_h[1, w] - half * (lead_k(ex) - ex - (green[k, 2, w + 1] - ez))
            green_h[2, w] = green_h[2, w] - half * (green[k, 1, w + 1] - ey - (lead_j(ex) - ex))
            return carry

        lax.fori_loop(reach - k, reach + 2 + k, one, 0)

    def green_electric(k):
        def one(w, carry):
            hx, hy, hz = green_h[0, w], green_h[1, w], green_h[2, w]
            green[k, 0, w] = green_rates[0, w - 1] * green[k - 1, 0, w] + green_rates[3, w - 1] * (
                0.5 * (hz - lag_j(hz) - (hy - lag_k(hy)))
            )
            green[k, 1, w] = green_rates[1, w - 1] * green[k - 1, 1, w] + green_rates[4, w - 1] * (
                0.5 * (hx - lag_k(hx) - (hz - green_h[2, w - 1]))
            )
            green[k, 2, w] = green_rates[2, w - 1] * green[k - 1, 2, w] + green_rates[5, w - 1] * (
                0.5 * (hy - green_h[1, w - 1] - (hx - lag_j(hx)))
            )
            return carry

        lax.fori_loop(reach + 1 - k, reach + 2 + k, one, 0)

    mon_at = monitor - me * width
    mon_ok = jnp.where((mon_at >= 0) & (mon_at < width), 1.0, 0.0)
    mon_at = jnp.clip(mon_at, 0, width - 1)

    def monitored(n):
        prod = hist[0, n + 1, 1, mon_at] * mon_ref[...]
        mid_own[pl.ds(n, 1)] = jnp.sum(prod, axis=0, keepdims=True) * mon_ok

    def step(n, carry):
        for r in range(2):
            electric_inner(r, n)
        green_magnetic(n)
        green_electric(n + 1)
        for r in range(2):
            wait_right(r, n)
            electric_first(r, n)
            wait_left(r, n)
            magnetic_last(r, n)
            magnetic_inner(r, n, 0)
            make_edge(r, n + 1)
            start_edge(r, n + 1)
        for r in range(2):
            for l in range(1, last):
                magnetic_inner(r, n, l)
        monitored(n)
        return carry

    lax.fori_loop(0, STEPS - 1, step, 0)
    n = STEPS - 1
    electric_inner(0, n)
    wait_right(0, n)
    electric_first(0, n)

    src_at = source - me * width
    src_ok = jnp.where((src_at >= 0) & (src_at < width), 1.0 / (rows * lanes), 0.0)
    src_at = jnp.clip(src_at, 0, width - 1)
    monitored(n)
    for f in range(NF):
        re = jnp.zeros((rows, lanes), jnp.float32)
        im = jnp.zeros((rows, lanes), jnp.float32)
        for t in range(STEPS):
            field = hist[0, t + 1, 2, src_at]
            re = re + cos_t[f, t : t + 1] * field
            im = im - sin_t[f, t : t + 1] * field
        mid_own[STEPS + f : STEPS + f + 1] = (
            jnp.sum(re * re + im * im, axis=0, keepdims=True) * src_ok
        )
    mid_own[STEPS + NF :] = jnp.zeros((16 - STEPS - NF, lanes), jnp.float32)
    mid_begin()
    mids[me] = mid_own[...]
    electric_inner(1, n)
    wait_right(1, n)
    electric_first(1, n)
    mid_end()

    def add_mid(s, acc):
        return acc + mids[s]

    total = lax.fori_loop(1, nd, add_mid, mids[0])
    total = jnp.broadcast_to(jnp.sum(total, axis=1, keepdims=True), (16, lanes))
    root = 1.0 / math.sqrt(rows * lanes)
    amp = []
    for f in range(NF):
        scale = root / jnp.sqrt(total[STEPS + f : STEPS + f + 1] + 1e-06)
        re = jnp.zeros((1, lanes), jnp.float32)
        im = jnp.zeros((1, lanes), jnp.float32)
        for t in range(STEPS):
            re = re + cos_t[f, t : t + 1] * total[t : t + 1]
            im = im - sin_t[f, t : t + 1] * total[t : t + 1]
        amp.append((re * scale, im * scale))
    drive = []
    for t in range(STEPS):
        s = jnp.zeros((1, lanes), jnp.float32)
        for f in range(NF):
            s = s + amp[f][0] * cos_t[f, t : t + 1] + amp[f][1] * sin_t[f, t : t + 1]
        drive.append(jnp.broadcast_to(s, (8, lanes)))

    for l in range(width):
        w = me * width + l - monitor + reach + 1
        w = jnp.where((w >= 1) & (w <= 2 * reach + 1), w, 0)

        def correlate(i, carry, l=l, w=w):
            c = lax.div(i, blocks)
            b = lax.rem(i, blocks)
            at = pl.ds(pl.multiple_of(b * 8, 8), 8)
            first = [hist[0, t + 1, c, l, at] for t in range(STEPS)]
            impulse = [green[t, c, w, at] for t in range(STEPS)]
            second = []
            for t in range(STEPS):
                a = hist[1, t + 1, c, l, at]
                for m in range(t + 1):
                    a = a + drive[m] * impulse[t - m]
                second.append(a)
            perm = jnp.zeros((8, lanes), jnp.float32)
            cond = jnp.zeros((8, lanes), jnp.float32)
            for p in range(2 * STEPS - 1):
                q = None
                for t in range(max(0, p - STEPS + 1), min(p, STEPS - 1) + 1):
                    term = first[t] * second[p - t]
                    q = term if q is None else q + term
                perm = perm + corr[0, p + 1 : p + 2] * q
                cond = cond + corr[1, p + 1 : p + 2] * q
            cells[c, l, pl.ds(b, 1)] = jnp.sum(perm, axis=0, keepdims=True)
            cells[3 + c, l, pl.ds(b, 1)] = jnp.sum(cond, axis=0, keepdims=True)
            return carry

        lax.fori_loop(0, 3 * blocks, correlate, 0, unroll=2)

    left = lax.broadcasted_iota(jnp.int32, (lanes, lanes), 0)
    up = lax.broadcasted_iota(jnp.int32, (lanes, lanes), 1)
    pool = (lax.div(left, 8) == lax.div(up, 8)).astype(jnp.float32)
    flat = cells[...].reshape(6 * width * blocks, lanes)
    pooled = jnp.dot(flat, pool, precision=HIGH, preferred_element_type=jnp.float32)
    pooled = pooled.reshape(6 * width, blocks, lanes)
    sub = lax.broadcasted_iota(jnp.int32, (blocks, lanes), 0)
    lane = lax.broadcasted_iota(jnp.int32, (blocks, lanes), 1)
    mine = lax.rem(lane, 8) == sub
    packed = jnp.sum(jnp.where(mine[None], pooled, 0.0), axis=1).reshape(6, width, lanes)
    region = lax.broadcasted_iota(jnp.int32, (regions, lanes), 0)
    partial = jnp.zeros((8, regions), jnp.float32)
    for l in range(width):
        hot = (region == jnp.broadcast_to(
                fact_own[1 + l : 2 + l].astype(jnp.int32), (regions, lanes)
            )).astype(
            jnp.float32
        )
        these = jnp.concatenate([packed[:, l], jnp.zeros((2, lanes), jnp.float32)], axis=0)
        partial = partial + lax.dot_general(
            these, hot, (((1,), (1,)), ((), ())), precision=HIGH, preferred_element_type=jnp.float32
        )
    end_own[...] = partial * math.sqrt(regions / (layers * rows * lanes))
    end_begin()
    ends[me] = end_own[...]
    end_end()

    def add_end(s, acc):
        return acc + ends[s]

    summed = lax.fori_loop(1, nd, add_end, ends[0])
    chosen = lax.broadcasted_iota(jnp.int32, (regions, lanes), 0)
    wanted = lax.broadcasted_iota(jnp.int32, (regions, lanes), 1) + me * per
    pick = ((chosen == wanted) & (wanted < (me + 1) * per)).astype(jnp.float32)
    mine = jnp.dot(summed, pick, precision=HIGH, preferred_element_type=jnp.float32)
    out_ref[...] = mine[:6, :per]

    for r in range(2):

        def done(n, carry, r=r):
            @pl.when(me < nd - 1)
            def _():
                right_copy(r, n).wait_send()

            @pl.when((me > 0) & (n < STEPS - 1))
            def _():
                left_copy(r, n).wait_send()

            return carry

        lax.fori_loop(0, STEPS, done, 0)


def local(nd, e, h, ae, ah, perm, cond, labels, source, monitor, wave, src_mode, mon_mode):
    width, blocks = labels.shape[0], labels.shape[1]
    rows, lanes = src_mode.shape
    per = perm.shape[1]
    regions = nd * per
    f32 = jnp.float32
    span = 2 * (STEPS - 1) + 1
    smem = pl.BlockSpec(memory_space=pltpu.SMEM)
    vmem = pl.BlockSpec(memory_space=pltpu.VMEM)
    hbm = pl.BlockSpec(memory_space=pl.ANY)
    dma = pltpu.SemaphoreType.DMA
    edge = pltpu.VMEM((2, STEPS, 2, rows, lanes), f32)
    out = pl.pallas_call(
        functools.partial(kernel, nd),
        out_shape=jax.ShapeDtypeStruct((6, per), f32),
        in_specs=[smem, smem, smem, hbm, hbm, hbm, hbm, vmem, vmem, vmem, vmem, vmem],
        out_specs=vmem,
        scratch_shapes=[
            pltpu.VMEM((2, STEPS + 1, 3, width, rows, lanes), f32),
            pltpu.VMEM((2, 3, width, rows, lanes), f32),
            edge,
            edge,
            edge,
            edge,
            pltpu.VMEM((6, width, rows, lanes), f32),
            pltpu.VMEM((2, rows, lanes), f32),
            pltpu.VMEM((STEPS, 3, span + 2, rows, lanes), f32),
            pltpu.VMEM((3, span + 2, rows, lanes), f32),
            pltpu.VMEM((6, span, rows, lanes), f32),
            pltpu.VMEM((nd, 8, lanes), f32),
            pltpu.VMEM((nd, 16, lanes), f32),
            pltpu.VMEM((nd, 8, regions), f32),
            pltpu.VMEM((6, width, blocks, lanes), f32),
            pltpu.VMEM((8, regions), f32),
            pltpu.VMEM((8, lanes), f32),
            pltpu.VMEM((1 + width, 8, lanes), f32),
            pltpu.VMEM((NF, 16, lanes), f32),
            pltpu.VMEM((NF, 16, lanes), f32),
            pltpu.VMEM((3, 16, lanes), f32),
            pltpu.VMEM((16, lanes), f32),
            pltpu.VMEM((8, regions), f32),
            dma((4,)),
            dma((2, STEPS)),
            dma((2, STEPS)),
            dma((2, STEPS)),
            dma((2, STEPS)),
            dma((3, nd)),
            dma((3, nd)),
        ],
        compiler_params=pltpu.CompilerParams(
            collective_id=0, has_side_effects=True, vmem_limit_bytes=60 * 1024 * 1024
        ),
    )(source, monitor, wave, e, h, ae, ah, perm, cond, labels, src_mode, mon_mode)
    return out


def solution(mesh):
    placed = (
        P(None, ("design", "domain"), None, None),
        P(None, ("design", "domain"), None, None),
        P(None, ("design", "domain"), None, None),
        P(None, ("design", "domain"), None, None),
        P(None, ("design", "domain")),
        P(None, ("design", "domain")),
        P(("design", "domain"), None, None),
        P("design"),
        P("design"),
        P("design"),
        P("design", None),
        P("design", None),
    )
    return jax.shard_map(
        functools.partial(local, mesh.shape["domain"]),
        mesh=mesh,
        in_specs=placed,
        out_specs=P(None, ("design", "domain")),
        check_vma=False,
    )
```
